32 devices in a mesh: dp: 8 (over y, x, core), tensor: 4 (over z).
Axes of the slice: x: 2, y: 2, z: 4, core: 2. Of those that a mesh axis runs over, the one named last changes fastest.
Arguments:
- hidden_in: bfloat16 [8, 1024, 1024], P('dp', 'tensor'), may hold values from -40 to 40
- segment_ids: int32 [8, 1024], P('dp'), may hold values from 0 to 1024, as said below
- gain_attn: float32 [1024], replicated, may hold values from 0.25 to 1.75
- gain_mlp: float32 [1024], replicated, may hold values from 0.25 to 1.75
- w_qkv: bfloat16 [1024, 3, 1024], P(None, None, 'tensor'), may hold values from -3 to 3
- w_out: bfloat16 [1024, 1024], P('tensor'), may hold values from -0.75 to 0.75
- w_in: bfloat16 [1024, 2, 2624], P(None, None, 'tensor'), may hold values from -0.1875 to 0.1875
- w_down: bfloat16 [2624, 1024], P('tensor'), may hold values from -0.125 to 0.125
- out_grad: bfloat16 [8, 1024, 1024], P('dp', 'tensor'), may hold values from -24 to 24
Outputs:
- hidden_out: bfloat16 [8, 1024, 1024], P('dp', 'tensor')
- hidden_grad: float32 [8, 1024, 1024], P('dp', 'tensor')
- gain_attn_grad: float32 [1024], P('tensor')
- gain_mlp_grad: float32 [1024], P('tensor')
- w_qkv_grad: float32 [1024, 3, 1024], P(None, None, 'tensor')
- w_out_grad: float32 [1024, 1024], P('tensor')
- w_in_grad: float32 [1024, 2, 2624], P(None, None, 'tensor')
- w_down_grad: float32 [2624, 1024], P('tensor')
The draws below stay inside these ranges and needn't reach their ends.
Inputs may be any that keep to these rules, and one draw needn't show every extreme that they name: `segment_ids`: within a group the ids never fall along the slots; documents carry ids 0, 1, 2 and so on in order; the id 1024 marks padding, which fills the last slots of every group, one or more of them.
All inputs are finite; a program needn't handle non-finite values.
Results may differ from the reference program's by a relative error of at most 0.035.
Values may be sent and summed in bfloat16 or wider, within the bound.
A program may use at most 128 MiB of HBM per device.

```python
import math
import jax
import jax.numpy as jnp
from jax import lax

D = 1024
HEADS = 16
HEAD_DIM = 64
FF = 2624
LEN_MAX = 512
GROUP_TOK = 1024
GROUPS = 8
N_TENSOR = 4


def draw_hidden_in(key, part):
    base_key = jax.random.fold_in(key, 11)
    col_key = jax.random.fold_in(base_key, 0)
    main_key = jax.random.fold_in(base_key, 2)
    col_scale = jnp.exp(jax.random.uniform(col_key, (D,), jnp.float32, math.log(0.3), math.log(3.0)))
    main_draw = jnp.clip(jax.random.normal(main_key, (GROUPS, GROUP_TOK, D), jnp.float32), -6.0, 6.0)
    field_vals = main_draw * col_scale
    return field_vals.astype(jnp.bfloat16)


def draw_segment_ids(key, part):
    base_key = jax.random.fold_in(key, 23)
    len_key, fill_key = jax.random.split(base_key, 2)
    doc_lens = jax.random.randint(len_key, (GROUPS, GROUP_TOK), 1, LEN_MAX + 1, dtype=jnp.int32)
    doc_lens = doc_lens.at[:, 0].set(jnp.maximum(doc_lens[:, 0], 4))
    doc_ends = jnp.cumsum(doc_lens, axis=1)
    token_idx = jnp.arange(GROUP_TOK, dtype=jnp.int32)
    seg_vals = jax.vmap(lambda ends_row: jnp.searchsorted(ends_row, token_idx, side='right'))(doc_ends).astype(jnp.int32)
    fill_len = jax.random.randint(fill_key, (GROUPS, 1), GROUP_TOK // 2, GROUP_TOK - 15, dtype=jnp.int32)
    return jnp.where(token_idx[None, :] < fill_len, seg_vals, GROUP_TOK).astype(jnp.int32)


def draw_w_qkv(key, part):
    base_vals = jnp.clip(jax.random.normal(jax.random.fold_in(key, 31), (D, 3, D), jnp.float32), -6.0, 6.0) * (1.0 / math.sqrt(D))
    return base_vals.astype(jnp.bfloat16)


def draw_out_grad(key, part):
    base_key = jax.random.fold_in(key, 41)
    main_key = jax.random.fold_in(base_key, 0)
    row_pos = jnp.arange(GROUPS * GROUP_TOK, dtype=jnp.float32).reshape(GROUPS, GROUP_TOK, 1)
    rise_vals = 1.0 + 2.0 * row_pos / (GROUPS * GROUP_TOK - 1)
    main_draw = jnp.clip(jax.random.normal(main_key, (GROUPS, GROUP_TOK, D), jnp.float32), -6.0, 6.0)
    grad_vals = main_draw * rise_vals
    return grad_vals.astype(jnp.bfloat16)


def block_scale(own_key, shape, pieces, least, top_value):
    factor_of = 1.0
    for position, blocks in pieces:
        draws = jax.random.uniform(jax.random.fold_in(jax.random.fold_in(own_key, 6), position), (blocks,), jnp.float32, least / len(pieces), top_value / len(pieces))
        factor_of = factor_of * jnp.repeat(jnp.exp(draws), shape[position] // blocks).reshape((-1,) + (1,) * (len(shape) - 1 - position))
    return factor_of


def gaussian(own_key, shape, scale, reach, cuts=(), held_as=jnp.bfloat16):
    values = scale * jax.random.normal(own_key, shape, jnp.float32)
    if cuts:
        values = values * block_scale(own_key, shape, cuts, -0.22, 0.18)
    return jnp.clip(values, -reach, reach).astype(held_as)


def setup_inputs(seed: int = 0) -> dict:
    arg_keys = jax.random.split(jax.random.key(seed), 10)
    return {
        "hidden_in": draw_hidden_in(jax.random.fold_in(arg_keys[9], 71), 0),
        "segment_ids": draw_segment_ids(jax.random.fold_in(arg_keys[9], 71), 0),
        "gain_attn": jnp.clip(1.0 + 0.15 * jax.random.normal(arg_keys[2], (D,), jnp.float32), 0.25, 1.75),
        "gain_mlp": jnp.clip(1.0 + 0.15 * jax.random.normal(arg_keys[3], (D,), jnp.float32), 0.25, 1.75),
        "w_qkv": draw_w_qkv(jax.random.fold_in(arg_keys[9], 71), 0),
        "w_out": gaussian(arg_keys[5], (D, D), 64 ** -0.5, 0.75, ((0, 4),)),
        "w_in": gaussian(arg_keys[6], (D, 2, FF), D ** -0.5, 0.1875, ((2, 4),)),
        "w_down": gaussian(arg_keys[7], (FF, D), FF ** -0.5, 0.125, ((0, 4),)),
        "out_grad": draw_out_grad(jax.random.fold_in(arg_keys[9], 71), 0),
    }


eps_norm = 1e-05
rope_theta = 160000.0
neg_fill = -1e+30
sqrt_half = 0.7071067811865476
inv_sqrt_two_pi = 0.3989422804014327

def norm_fwd(rows_f, gain_vec):
    mean_row = lax.optimization_barrier(jnp.mean(rows_f, axis=-1, keepdims=True))
    centred = rows_f - mean_row
    var_row = lax.optimization_barrier(jnp.mean(centred * centred, axis=-1, keepdims=True))
    inv_std = lax.rsqrt(var_row + eps_norm)
    hat_rows = centred * inv_std
    return ((hat_rows * gain_vec).astype(jnp.bfloat16), hat_rows, inv_std)

def norm_bwd(grad_norm, hat_rows, inv_std, gain_vec):
    grad_hat = grad_norm * gain_vec
    mean_one = lax.optimization_barrier(jnp.mean(grad_hat, axis=-1, keepdims=True))
    mean_two = lax.optimization_barrier(jnp.mean(grad_hat * hat_rows, axis=-1, keepdims=True))
    return inv_std * (grad_hat - mean_one - hat_rows * mean_two)

def half_turn(field_in):
    half_dim = field_in.shape[-1] // 2
    return jnp.concatenate([-field_in[..., half_dim:], field_in[..., :half_dim]], axis=-1)

def positions_of(seg_row):
    before = lax.optimization_barrier(jnp.sum((seg_row[None, :] < seg_row[:, None]).astype(jnp.int32), axis=1))
    return jnp.arange(seg_row.shape[0], dtype=jnp.int32) - before

def rope_tables(positions, head_dim):
    half_dim = head_dim // 2
    inv_freq = jnp.exp(jnp.arange(half_dim, dtype=jnp.float32) * (-2.0 * math.log(rope_theta) / head_dim))
    angles = positions.astype(jnp.float32)[:, None] * inv_freq[None, :]
    cos_tab = jnp.concatenate([jnp.cos(angles), jnp.cos(angles)], axis=-1)
    sin_tab = jnp.concatenate([jnp.sin(angles), jnp.sin(angles)], axis=-1)
    return (cos_tab[:, None, :], sin_tab[:, None, :])

def rope_apply(field_in, cos_tab, sin_tab):
    return field_in * cos_tab + half_turn(field_in) * sin_tab

def rope_back(grad_in, cos_tab, sin_tab):
    return grad_in * cos_tab - half_turn(grad_in * sin_tab)

def gelu_val(field_in):
    return 0.5 * field_in * (1.0 + lax.erf(field_in * sqrt_half))

def gelu_slope(field_in):
    return 0.5 * (1.0 + lax.erf(field_in * sqrt_half)) + field_in * jnp.exp(-0.5 * field_in * field_in) * inv_sqrt_two_pi

def blocked_sum(left, right, spec):
    parts = jnp.einsum(spec, left.astype(jnp.float32), right.astype(jnp.float32))
    rounded = lax.optimization_barrier(parts.astype(jnp.bfloat16))
    return lax.optimization_barrier(jnp.sum(rounded.astype(jnp.float32), axis=0))

def attend_fwd(queries, key_rows, value_rows, seg_row):
    total_rows = queries.shape[0]
    block_rows = min(512, total_rows)
    scale_val = 1.0 / math.sqrt(queries.shape[2])
    key_f = key_rows.astype(jnp.float32)
    value_f = value_rows.astype(jnp.float32)

    def one_block(block_idx):
        start_row = block_idx * block_rows
        query_blk = lax.dynamic_slice_in_dim(queries, start_row, block_rows, 0).astype(jnp.float32)
        seg_blk = lax.dynamic_slice_in_dim(seg_row, start_row, block_rows, 0)
        scores = jnp.einsum('qhd,khd->hqk', query_blk, key_f) * scale_val
        same_doc = seg_blk[:, None] == seg_row[None, :]
        scores = jnp.where(same_doc[None], scores, neg_fill)
        row_top = lax.optimization_barrier(jnp.max(scores, axis=-1, keepdims=True))
        exp_vals = jnp.exp(scores - row_top)
        row_total = lax.optimization_barrier(jnp.sum(exp_vals, axis=-1, keepdims=True))
        prob_bf = (exp_vals / row_total).astype(jnp.bfloat16)
        out_blk = jnp.einsum('hqk,khd->qhd', prob_bf.astype(jnp.float32), value_f).astype(jnp.bfloat16)
        return (out_blk, (row_top + jnp.log(row_total))[..., 0])
    out_blocks, lse_blocks = lax.map(one_block, jnp.arange(total_rows // block_rows, dtype=jnp.int32))
    head_count = queries.shape[1]
    att_out = out_blocks.reshape(total_rows, head_count, queries.shape[2])
    lse_rows = jnp.transpose(lse_blocks, (1, 0, 2)).reshape(head_count, total_rows)
    return (att_out, lse_rows)

def attend_bwd(queries, key_rows, value_rows, seg_row, att_out, grad_att, lse_rows):
    total_rows = queries.shape[0]
    block_rows = min(512, total_rows)
    scale_val = 1.0 / math.sqrt(queries.shape[2])
    key_f = key_rows.astype(jnp.float32)
    value_f = value_rows.astype(jnp.float32)
    delta_rows = lax.optimization_barrier(jnp.sum(grad_att.astype(jnp.float32) * att_out.astype(jnp.float32), axis=-1))

    def one_block(acc_pair, block_idx):
        grad_key, grad_value = acc_pair
        start_row = block_idx * block_rows
        query_blk = lax.dynamic_slice_in_dim(queries, start_row, block_rows, 0).astype(jnp.float32)
        grad_blk = lax.dynamic_slice_in_dim(grad_att, start_row, block_rows, 0).astype(jnp.float32)
        seg_blk = lax.dynamic_slice_in_dim(seg_row, start_row, block_rows, 0)
        delta_blk = lax.dynamic_slice_in_dim(delta_rows, start_row, block_rows, 0)
        lse_blk = lax.dynamic_slice_in_dim(lse_rows, start_row, block_rows, 1)
        scores = jnp.einsum('qhd,khd->hqk', query_blk, key_f) * scale_val
        same_doc = seg_blk[:, None] == seg_row[None, :]
        scores = jnp.where(same_doc[None], scores, neg_fill)
        prob_f = jnp.exp(scores - lse_blk[:, :, None])
        grad_prob = jnp.einsum('qhd,khd->hqk', grad_blk, value_f)
        grad_score = prob_f * (grad_prob - jnp.transpose(delta_blk)[:, :, None])
        prob_bf = prob_f.astype(jnp.bfloat16).astype(jnp.float32)
        score_bf = grad_score.astype(jnp.bfloat16).astype(jnp.float32)
        grad_value = grad_value + jnp.einsum('hqk,qhd->khd', prob_bf, grad_blk)
        grad_key = grad_key + jnp.einsum('hqk,qhd->khd', score_bf, query_blk) * scale_val
        grad_query_blk = jnp.einsum('hqk,khd->qhd', score_bf, key_f) * scale_val
        return ((grad_key, grad_value), grad_query_blk)
    zero_rows = jnp.zeros(key_rows.shape, jnp.float32)
    acc_pair, query_blocks = lax.scan(one_block, (zero_rows, zero_rows), jnp.arange(total_rows // block_rows, dtype=jnp.int32))
    return (query_blocks.reshape(queries.shape), acc_pair[0], acc_pair[1])

def reference(hidden_in, segment_ids, gain_attn, gain_mlp, w_qkv, w_out, w_in, w_down, out_grad):
    n_parts = N_TENSOR
    width_local = D // n_parts
    ff_local = FF // n_parts
    total_rows = GROUP_TOK

    def group_step(carried, group_items):
        rows_in, seg_row, grad_rows = group_items
        positions = positions_of(seg_row)
        cos_tab, sin_tab = rope_tables(positions, HEAD_DIM)
        valid_rows = (seg_row < GROUP_TOK).astype(jnp.float32)
        rows_f = rows_in.astype(jnp.float32)
        normed_attn, hat_attn, inv_attn = norm_fwd(rows_f, gain_attn)
        projected = jnp.dot(normed_attn, w_qkv.reshape(D, 3 * D), preferred_element_type=jnp.float32)
        projected = projected.reshape(total_rows, 3, HEADS, HEAD_DIM)
        queries = rope_apply(projected[:, 0], cos_tab, sin_tab).astype(jnp.bfloat16)
        key_rows = rope_apply(projected[:, 1], cos_tab, sin_tab).astype(jnp.bfloat16)
        value_rows = projected[:, 2].astype(jnp.bfloat16)
        att_out, lse_rows = attend_fwd(queries, key_rows, value_rows, seg_row)
        att_flat = att_out.reshape(total_rows, D)
        att_sum = blocked_sum(att_flat.reshape(total_rows, n_parts, width_local), w_out.reshape(n_parts, width_local, D), 'snk,nkd->nsd')
        mid_rows = rows_f + att_sum
        normed_mlp, hat_mlp, inv_mlp = norm_fwd(mid_rows, gain_mlp)
        pre_act = jnp.dot(normed_mlp, w_in.reshape(D, 2 * FF), preferred_element_type=jnp.float32).reshape(total_rows, 2, FF)
        up_part = pre_act[:, 0]
        gate_part = pre_act[:, 1]
        act_up = gelu_val(up_part)
        mixed_act = (act_up * gate_part).astype(jnp.bfloat16)
        mlp_sum = blocked_sum(mixed_act.reshape(total_rows, n_parts, ff_local), w_down.reshape(n_parts, ff_local, D), 'snk,nkd->nsd')
        final_rows = (mid_rows + mlp_sum).astype(jnp.bfloat16)
        grad_top = grad_rows.astype(jnp.float32) * valid_rows[:, None]
        grad_top_bf = grad_top.astype(jnp.bfloat16)
        grad_down = jnp.dot(mixed_act.T, grad_top_bf, preferred_element_type=jnp.float32)
        d_mixed = jnp.dot(grad_top_bf, w_down.T, preferred_element_type=jnp.float32)
        d_up = d_mixed * gate_part * gelu_slope(up_part)
        d_gate = d_mixed * act_up
        d_pre = jnp.stack([d_up, d_gate], axis=1).astype(jnp.bfloat16)
        grad_in = jnp.dot(normed_mlp.T, d_pre.reshape(total_rows, 2 * FF), preferred_element_type=jnp.float32).reshape(D, 2, FF)
        d_norm_mlp = blocked_sum(d_pre.reshape(total_rows, 2, n_parts, ff_local), w_in.reshape(D, 2, n_parts, ff_local), 'scnf,dcnf->nsd')
        gain_mlp_part = lax.optimization_barrier(jnp.sum(d_norm_mlp * hat_mlp, axis=0))
        d_mid = grad_top + norm_bwd(d_norm_mlp, hat_mlp, inv_mlp, gain_mlp)
        d_mid_bf = d_mid.astype(jnp.bfloat16)
        grad_out_w = jnp.dot(att_flat.T, d_mid_bf, preferred_element_type=jnp.float32)
        d_att = jnp.dot(d_mid_bf, w_out.T, preferred_element_type=jnp.float32).astype(jnp.bfloat16)
        d_att = d_att.reshape(total_rows, HEADS, HEAD_DIM)
        grad_query, grad_key, grad_value = attend_bwd(queries, key_rows, value_rows, seg_row, att_out, d_att, lse_rows)
        grad_query = rope_back(grad_query, cos_tab, sin_tab)
        grad_key = rope_back(grad_key, cos_tab, sin_tab)
        d_proj = jnp.stack([grad_query, grad_key, grad_value], axis=1).reshape(total_rows, 3, D).astype(jnp.bfloat16)
        grad_qkv = jnp.dot(normed_attn.T, d_proj.reshape(total_rows, 3 * D), preferred_element_type=jnp.float32).reshape(D, 3, D)
        d_norm_attn = blocked_sum(d_proj.reshape(total_rows, 3, n_parts, width_local), w_qkv.reshape(D, 3, n_parts, width_local), 'scnf,dcnf->nsd')
        gain_attn_part = lax.optimization_barrier(jnp.sum(d_norm_attn * hat_attn, axis=0))
        d_rows = d_mid + norm_bwd(d_norm_attn, hat_attn, inv_attn, gain_attn)
        acc_qkv, acc_out, acc_in, acc_down, acc_gain_attn, acc_gain_mlp = carried
        carried = (acc_qkv + grad_qkv, acc_out + grad_out_w, acc_in + grad_in, acc_down + grad_down, acc_gain_attn + gain_attn_part, acc_gain_mlp + gain_mlp_part)
        return (carried, (final_rows, d_rows))
    start_acc = (jnp.zeros((D, 3, D), jnp.float32), jnp.zeros((D, D), jnp.float32), jnp.zeros((D, 2, FF), jnp.float32), jnp.zeros((FF, D), jnp.float32), jnp.zeros((D,), jnp.float32), jnp.zeros((D,), jnp.float32))
    carried, (outs_all, grads_all) = lax.scan(group_step, start_acc, (hidden_in, segment_ids, out_grad))
    acc_qkv, acc_out, acc_in, acc_down, acc_gain_attn, acc_gain_mlp = carried
    return (outs_all, grads_all, acc_gain_attn, acc_gain_mlp, acc_qkv, acc_out, acc_in, acc_down)
```

```python
import functools
import math

import jax
import jax.numpy as jnp
from jax import lax
from jax.experimental import pallas as pl
from jax.experimental.pallas import tpu as pltpu
from jax.sharding import PartitionSpec as P


HEAD_DIM = 64


eps_norm = 1e-05
rope_theta = 160000.0
neg_fill = -1e30
sqrt_half = 0.7071067811865476
inv_sqrt_two_pi = 0.3989422804014327


def norm_fwd(rows_f, gain_vec):
    mean_row = jnp.mean(rows_f, axis=-1, keepdims=True)
    centred = rows_f - mean_row
    var_row = jnp.mean(centred * centred, axis=-1, keepdims=True)
    inv_std = lax.rsqrt(var_row + eps_norm)
    hat_rows = centred * inv_std
    return ((hat_rows * gain_vec).astype(jnp.bfloat16), hat_rows, inv_std)


def norm_bwd(grad_norm, hat_rows, inv_std, gain_vec):
    grad_hat = grad_norm * gain_vec
    mean_one = jnp.mean(grad_hat, axis=-1, keepdims=True)
    mean_two = jnp.mean(grad_hat * hat_rows, axis=-1, keepdims=True)
    return inv_std * (grad_hat - mean_one - hat_rows * mean_two)


def rope_tables(positions, head_dim):
    half_dim = head_dim // 2
    inv_freq = jnp.exp(
        jnp.arange(half_dim, dtype=jnp.float32) * (-2.0 * math.log(rope_theta) / head_dim)
    )
    angles = positions.astype(jnp.float32)[:, None] * inv_freq[None, :]
    cos_tab = jnp.concatenate([jnp.cos(angles), jnp.cos(angles)], axis=-1)
    sin_tab = jnp.concatenate([jnp.sin(angles), jnp.sin(angles)], axis=-1)
    return (cos_tab[None], sin_tab[None])


def gelu_val(field_in):
    return 0.5 * field_in * (1.0 + lax.erf(field_in * sqrt_half))


def gelu_slope(field_in):
    return (
        0.5 * (1.0 + lax.erf(field_in * sqrt_half))
        + field_in * jnp.exp(-0.5 * field_in * field_in) * inv_sqrt_two_pi
    )


def bit_orders(n_dp):
    bits = [1 << i for i in range(n_dp.bit_length() - 1)]
    rest = bits[1:]
    turn = len(rest) // 2
    return (bits, bits[:1] + rest[turn:] + rest[:turn])


def grad_reduce_kernel(n_dp, n_tp, shifts, whole, *refs):
    orders = bit_orders(n_dp)
    n_stage = len(orders[0])
    n_arr = len(shifts)
    x_refs = refs[:n_arr]
    out_refs = refs[n_arr : 2 * n_arr]
    pos = 2 * n_arr
    gath = refs[pos : pos + n_arr]
    pos += n_arr
    recv, work, far = {}, {}, {}
    for arr in range(n_arr):
        if whole[arr]:
            for stage in range(n_stage):
                recv[arr, stage] = refs[pos]
                pos += 1
            for stage in range(n_stage):
                work[arr, stage] = refs[pos]
                pos += 1
        if len(shifts[arr]) > 1:
            far[arr] = refs[pos]
            pos += 1
    send_sem, recv_sem, far_send, far_recv = refs[pos : pos + 4]
    me = lax.axis_index("dp")
    mine = lax.axis_index("tensor")
    mesh_type = pl.DeviceIdType.MESH

    def bit_of(bit):
        return lax.rem(me // bit, 2)

    def partner_of(bit):
        return me + bit - 2 * bit * bit_of(bit)

    pending = []

    def remote(src, dst, step, half, arr, bit):
        copy = pltpu.make_async_remote_copy(
            src_ref=src,
            dst_ref=dst,
            send_sem=send_sem.at[step, half, arr],
            recv_sem=recv_sem.at[step, half, arr],
            device_id=(partner_of(bit), mine),
            device_id_type=mesh_type,
        )
        copy.start()
        pending.append(copy)
        return copy

    steps = {s for row in shifts for s in row if s}
    steps = sorted(steps | {n_tp - s for s in steps})
    barrier = pltpu.get_barrier_semaphore()
    for bit in orders[0]:
        pl.semaphore_signal(barrier, inc=1, device_id=(partner_of(bit), mine), device_id_type=mesh_type)
    for s in steps:
        pl.semaphore_signal(
            barrier, inc=1, device_id=(me, lax.rem(mine + s, n_tp)), device_id_type=mesh_type
        )
    pl.semaphore_wait(barrier, n_stage + len(steps))

    offs = [[0], [0]]
    for half in range(2):
        for stage in range(n_stage):
            bit = orders[half][stage]
            offs[half].append(offs[half][-1] + bit_of(bit) * (n_dp >> (stage + 1)))

    def source(arr, stage):
        return x_refs[arr] if stage == 0 else work[arr, stage - 1]

    def start_sum(arr, half, stage):
        bit = orders[half][stage]
        size = n_dp >> (stage + 1)
        away = (1 - bit_of(bit)) * size
        src = source(arr, stage).at[half, pl.ds(away, size)]
        return remote(src, recv[arr, stage].at[half], stage, half, arr, bit)

    def own_piece(arr, half):
        if whole[arr]:
            return work[arr, n_stage - 1].at[half, 0]
        return x_refs[arr].at[half, 0]

    def start_far(arr, half):
        part = gath[arr].shape[2]
        copies = []
        for b in range(1, len(shifts[arr])):
            copy = pltpu.make_async_remote_copy(
                src_ref=own_piece(arr, half).at[pl.ds(b * part, part)],
                dst_ref=far[arr].at[b - 1, half],
                send_sem=far_send.at[arr, b, half],
                recv_sem=far_recv.at[arr, b, half],
                device_id=(me, lax.rem(mine + shifts[arr][b], n_tp)),
                device_id_type=mesh_type,
            )
            copy.start()
            pending.append(copy)
            copies.append(copy)
        return copies

    def start_spread(arr, half, stage):
        size = n_dp >> (stage + 1)
        part = gath[arr].at[half, pl.ds(offs[half][stage + 1], size)]
        return remote(part, part, n_stage + stage, half, arr, orders[half][stage])

    def finish_sum(arr, half, stage, copy):
        size = n_dp >> (stage + 1)
        kept = bit_of(orders[half][stage]) * size
        copy.wait_recv()
        src, got, dst = source(arr, stage), recv[arr, stage], work[arr, stage]

        def add_one(i, carry):
            total = src[half, kept + i].astype(jnp.float32) + got[half, i].astype(jnp.float32)
            dst[half, i] = total.astype(jnp.bfloat16)
            return carry

        lax.fori_loop(0, size, add_one, 0)

    def finish_far(arr, half, copies):
        part = gath[arr].shape[2]
        total = own_piece(arr, half)[pl.ds(0, part)].astype(jnp.float32)
        for b, copy in enumerate(copies):
            copy.wait_recv()
            total = total + far[arr][b, half].astype(jnp.float32)
        gath[arr][half, offs[half][-1]] = total.astype(jnp.bfloat16)

    order = [(arr, half) for arr in range(n_arr) for half in range(2)]
    flying = {}
    for key in order:
        flying[key] = start_sum(*key, 0) if whole[key[0]] else start_far(*key)
    for stage in range(n_stage):
        for arr, half in order:
            if whole[arr]:
                finish_sum(arr, half, stage, flying[arr, half])
                if stage + 1 < n_stage:
                    flying[arr, half] = start_sum(arr, half, stage + 1)
                else:
                    flying[arr, half] = start_far(arr, half)
    for arr, half in order:
        finish_far(arr, half, flying[arr, half])
        flying[arr, half] = start_spread(arr, half, n_stage - 1)
    for stage in reversed(range(n_stage)):
        for arr, half in order:
            flying[arr, half].wait_recv()
            if stage:
                flying[arr, half] = start_spread(arr, half, stage - 1)
    for arr, half in order:
        if whole[arr]:

            def move_one(i, carry, arr=arr, half=half):
                out_refs[arr][half, i] = gath[arr][half, i].astype(out_refs[arr].dtype)
                return carry

            lax.fori_loop(0, n_dp, move_one, 0)
        else:
            for i in range(n_dp):
                slot = 0
                for stage in range(n_stage):
                    slot += (i // orders[half][stage]) % 2 * (n_dp >> (stage + 1))
                out_refs[arr][half, i] = gath[arr][half, slot].astype(out_refs[arr].dtype)
    for copy in pending:
        copy.wait_send()


def grad_reduce(grads, shifts, shares, share_shifts, call_id):
    n_dp = lax.axis_size("dp")
    n_tp = lax.axis_size("tensor")
    n_stage = n_dp.bit_length() - 1
    bf = jnp.bfloat16
    args, cols, parts, rows_of = [], [], [], []
    for blocks in grads:
        rows, c = blocks[0].shape
        full = padded(rows, 32 * n_dp)
        part = full // (2 * n_dp)
        args.append(
            jnp.concatenate(
                [with_rows(g, full).reshape(2, n_dp, part, c) for g in blocks], axis=2
            ).astype(bf)
        )
        cols.append(c)
        parts.append(part)
        rows_of.append(rows)
    for share, row in zip(shares, share_shifts):
        args.append(share)
        cols.append(share.shape[-1])
        parts.append(share.shape[2] // len(row))
    shifts = tuple(shifts) + tuple(share_shifts)
    whole = (True,) * len(grads) + (False,) * len(shares)
    scratch = [pltpu.VMEM((2, n_dp, p, c), bf) for p, c in zip(parts, cols)]
    for row, p, c, w in zip(shifts, parts, cols, whole):
        if w:
            for _ in range(2):
                for stage in range(n_stage):
                    scratch.append(pltpu.VMEM((2, n_dp >> (stage + 1), len(row) * p, c), bf))
        if len(row) > 1:
            scratch.append(pltpu.VMEM((len(row) - 1, 2, p, c), bf))
    most = max(len(row) for row in shifts)
    scratch += [pltpu.SemaphoreType.DMA((2 * n_stage, 2, len(args)))] * 2
    scratch += [pltpu.SemaphoreType.DMA((len(args), most, 2))] * 2
    moved = sum(4 * n_dp * len(row) * p * c for row, p, c in zip(shifts, parts, cols))
    done = pl.pallas_call(
        functools.partial(grad_reduce_kernel, n_dp, n_tp, shifts, whole),
        out_shape=[
            jax.ShapeDtypeStruct((2, n_dp, p, c), jnp.float32) for p, c in zip(parts, cols)
        ],
        in_specs=[pl.BlockSpec(memory_space=pltpu.VMEM)] * len(args),
        out_specs=[pl.BlockSpec(memory_space=pltpu.VMEM)] * len(args),
        scratch_shapes=scratch,
        cost_estimate=pl.CostEstimate(flops=0, bytes_accessed=30 * moved, transcendentals=0),
        compiler_params=pltpu.CompilerParams(
            collective_id=call_id, has_side_effects=True, vmem_limit_bytes=48 << 20
        ),
    )(*args)
    totals = [o.reshape(-1, c)[:rows] for o, c, rows in zip(done, cols, rows_of)]
    return totals, done[len(grads) :]


def gain_reduce_kernel(n_dp, n_tp, x_ref, out_ref, stage_buf, from_tp, from_dp, t_send, t_recv, d_send, d_recv, c_sem):
    me = lax.axis_index("dp")
    mine = lax.axis_index("tensor")
    mesh_type = pl.DeviceIdType.MESH
    barrier = pltpu.get_barrier_semaphore()
    for k in range(1, n_tp):
        pl.semaphore_signal(
            barrier, inc=1, device_id=(me, lax.rem(mine + k, n_tp)), device_id_type=mesh_type
        )
    for k in range(1, n_dp):
        pl.semaphore_signal(
            barrier, inc=1, device_id=(lax.rem(me + k, n_dp), mine), device_id_type=mesh_type
        )
    pl.semaphore_wait(barrier, n_tp + n_dp - 2)
    copies = []
    for k in range(1, n_tp):
        target = lax.rem(mine + k, n_tp)
        copies.append(
            pltpu.make_async_remote_copy(
                src_ref=x_ref.at[target],
                dst_ref=from_tp.at[k],
                send_sem=t_send.at[k],
                recv_sem=t_recv.at[k],
                device_id=(me, target),
                device_id_type=mesh_type,
            )
        )
        copies[-1].start()
    total = x_ref[mine]
    for k in range(1, n_tp):
        copies[k - 1].wait()
        total = total + from_tp[k]
    stage_buf[...] = total
    local = pltpu.make_async_copy(stage_buf, from_dp.at[0], c_sem)
    local.start()
    local.wait()
    copies = []
    for k in range(1, n_dp):
        copies.append(
            pltpu.make_async_remote_copy(
                src_ref=from_dp.at[0],
                dst_ref=from_dp.at[k],
                send_sem=d_send.at[k],
                recv_sem=d_recv.at[k],
                device_id=(lax.rem(me + k, n_dp), mine),
                device_id_type=mesh_type,
            )
        )
        copies[-1].start()
    for k in range(1, n_dp):
        copies[k - 1].wait()
        total = total + from_dp[k]
    out_ref[...] = total


def gain_reduce(parts, call_id):
    n_dp = lax.axis_size("dp")
    n_tp = lax.axis_size("tensor")
    wide = parts.shape[1] // n_tp
    arg = jnp.transpose(parts.reshape(2, n_tp, wide), (1, 0, 2))
    return pl.pallas_call(
        functools.partial(gain_reduce_kernel, n_dp, n_tp),
        out_shape=jax.ShapeDtypeStruct((2, wide), jnp.float32),
        in_specs=[pl.BlockSpec(memory_space=pltpu.VMEM)],
        out_specs=pl.BlockSpec(memory_space=pltpu.VMEM),
        scratch_shapes=[
            pltpu.VMEM((2, wide), jnp.float32),
            pltpu.VMEM((n_tp, 2, wide), jnp.float32),
            pltpu.VMEM((n_dp, 2, wide), jnp.float32),
            pltpu.SemaphoreType.DMA((n_tp,)),
            pltpu.SemaphoreType.DMA((n_tp,)),
            pltpu.SemaphoreType.DMA((n_dp,)),
            pltpu.SemaphoreType.DMA((n_dp,)),
            pltpu.SemaphoreType.DMA,
        ],
        cost_estimate=pl.CostEstimate(flops=0, bytes_accessed=20 << 20, transcendentals=0),
        compiler_params=pltpu.CompilerParams(collective_id=call_id, has_side_effects=True),
    )(arg)


def turn_lanes(field_in, half_dim):
    lanes = lax.broadcasted_iota(jnp.int32, field_in.shape, 1)
    width = field_in.shape[1]
    low = lanes % (2 * half_dim) < half_dim
    ahead = pltpu.roll(field_in, width - half_dim, 1)
    behind = pltpu.roll(field_in, half_dim, 1)
    return jnp.where(low, -ahead, behind)


def head_mask(shape, head):
    return lax.broadcasted_iota(jnp.int32, shape, 1) // HEAD_DIM == head


def dot_last(left, right):
    return lax.dot_general(left, right, (((1,), (1,)), ((), ())), preferred_element_type=jnp.float32)


def dot_mid(left, right):
    return lax.dot_general(left, right, (((1,), (0,)), ((), ())), preferred_element_type=jnp.float32)


def attn_fwd_kernel(n_blk, n_head, *refs):
    q_in, k_in, v_in = refs[:n_blk], refs[n_blk : 2 * n_blk], refs[2 * n_blk : 3 * n_blk]
    cos_ref, sin_ref, segc_ref, segr_ref = refs[3 * n_blk : 3 * n_blk + 4]
    q_ref, k_ref, v_ref, att_ref, lse_ref, vt_ref = refs[3 * n_blk + 4 :]
    blk = q_in[0].shape[0]
    half_dim = HEAD_DIM // 2
    scale_val = 1.0 / math.sqrt(HEAD_DIM)
    for c in range(n_blk):
        rows = pl.ds(c * blk, blk)
        cos_tab, sin_tab = cos_ref[rows], sin_ref[rows]
        for src, dst in ((q_in[c], q_ref), (k_in[c], k_ref)):
            z = src[...]
            dst[rows] = (z * cos_tab + turn_lanes(z, half_dim) * sin_tab).astype(jnp.bfloat16)
        value = v_in[c][...]
        v_ref[rows] = value.astype(jnp.bfloat16)
        vt_ref[:, rows] = jnp.transpose(value).astype(jnp.bfloat16)

    def one_block(i, carry):
        rows = pl.ds(pl.multiple_of(i * blk, blk), blk)
        query = q_ref[rows]
        same_doc = segc_ref[...] == segr_ref[:, rows]
        parts = []
        for h in range(n_head):
            masked = jnp.where(head_mask(query.shape, h), query, jnp.zeros_like(query))
            scores = jnp.where(same_doc, dot_last(k_ref[...], masked) * scale_val, neg_fill)
            top = jnp.max(scores, axis=0, keepdims=True)
            exp_vals = jnp.exp(scores - top)
            total = jnp.sum(exp_vals, axis=0, keepdims=True)
            prob_bf = (exp_vals * (1.0 / total)).astype(jnp.bfloat16)
            parts.append(dot_mid(vt_ref[h * HEAD_DIM : (h + 1) * HEAD_DIM], prob_bf))
            lse_ref[0, h : h + 1, rows] = top + jnp.log(total)
        out = jnp.transpose(jnp.concatenate(parts, axis=0))
        att_ref[rows] = out.astype(jnp.bfloat16)
        return carry

    lax.fori_loop(0, n_blk, one_block, 0)


def attn_bwd_kernel(n_blk, n_head, *refs):
    d_in = refs[:n_blk]
    q_ref, k_ref, v_ref, att_ref, lse_ref, cos_ref, sin_ref, segc_ref, segr_ref = refs[n_blk : n_blk + 9]
    out_ref, d_ref, kt_ref, dk_ref, dv_ref = refs[n_blk + 9 :]
    blk = d_in[0].shape[0]
    half_dim = HEAD_DIM // 2
    scale_val = 1.0 / math.sqrt(HEAD_DIM)
    for c in range(n_blk):
        rows = pl.ds(c * blk, blk)
        d_ref[rows] = d_in[c][...]
        kt_ref[:, rows] = jnp.transpose(k_ref[rows].astype(jnp.float32)).astype(jnp.bfloat16)
    dk_ref[...] = jnp.zeros_like(dk_ref)
    dv_ref[...] = jnp.zeros_like(dv_ref)

    def back_turn(grad, rows):
        turned = turn_lanes(grad * sin_ref[rows], half_dim)
        return (grad * cos_ref[rows] - turned).astype(jnp.bfloat16)

    def one_block(i, carry):
        rows = pl.ds(pl.multiple_of(i * blk, blk), blk)
        query, d_att = q_ref[rows], d_ref[rows]
        both = jnp.transpose(d_att.astype(jnp.float32) * att_ref[rows].astype(jnp.float32))
        same_doc = segc_ref[...] == segr_ref[:, rows]
        parts = []
        for h in range(n_head):
            own = head_mask(query.shape, h)
            q_h = jnp.where(own, query, jnp.zeros_like(query))
            d_h = jnp.where(own, d_att, jnp.zeros_like(d_att))
            delta = jnp.sum(both[h * HEAD_DIM : (h + 1) * HEAD_DIM], axis=0, keepdims=True)
            scores = jnp.where(same_doc, dot_last(k_ref[...], q_h) * scale_val, neg_fill)
            prob_f = jnp.exp(scores - lse_ref[0, h : h + 1, rows])
            grad_prob = dot_last(v_ref[...], d_h)
            score_bf = (prob_f * (grad_prob - delta)).astype(jnp.bfloat16)
            dv_ref[...] += dot_mid(prob_f.astype(jnp.bfloat16), d_h)
            dk_ref[...] += dot_mid(score_bf, q_h)
            parts.append(dot_mid(kt_ref[h * HEAD_DIM : (h + 1) * HEAD_DIM], score_bf))
        grad_query = jnp.transpose(jnp.concatenate(parts, axis=0)) * scale_val
        out_ref[0, rows] = back_turn(grad_query, rows)
        return carry

    lax.fori_loop(0, n_blk, one_block, 0)
    for c in range(n_blk):
        rows = pl.ds(c * blk, blk)
        out_ref[1, rows] = back_turn(dk_ref[rows] * scale_val, rows)
        out_ref[2, rows] = dv_ref[rows].astype(jnp.bfloat16)


def table_specs(rows, lanes):
    return [
        pl.BlockSpec((rows, lanes), lambda p: (0, 0)),
        pl.BlockSpec((rows, lanes), lambda p: (0, 0)),
        pl.BlockSpec((rows, 1), lambda p: (0, 0)),
        pl.BlockSpec((1, rows), lambda p: (0, 0)),
    ]


def attn_fwd(chunks, cos_tab, sin_tab, seg_row, width):
    n_blk, blk = len(chunks), chunks[0].shape[0]
    rows = n_blk * blk
    n_head = 2
    lanes = n_head * HEAD_DIM
    n_pair = width // lanes

    def at(s):
        return pl.BlockSpec((blk, lanes), lambda p: (0, s * n_pair + p))

    wide = pl.BlockSpec((rows, lanes), lambda p: (0, p))
    flat = jax.ShapeDtypeStruct((rows, width), jnp.bfloat16)
    return pl.pallas_call(
        functools.partial(attn_fwd_kernel, n_blk, n_head),
        grid=(n_pair,),
        in_specs=[at(s) for s in range(3) for _ in range(n_blk)] + table_specs(rows, lanes),
        out_specs=[wide, wide, wide, wide, pl.BlockSpec((1, n_head, rows), lambda p: (p, 0, 0))],
        out_shape=[flat] * 4 + [jax.ShapeDtypeStruct((n_pair, n_head, rows), jnp.float32)],
        scratch_shapes=[pltpu.VMEM((lanes, rows), jnp.bfloat16)],
        cost_estimate=pl.CostEstimate(
            flops=4 * rows * rows * width, bytes_accessed=24 * rows * width, transcendentals=rows * rows * width // HEAD_DIM
        ),
        compiler_params=pltpu.CompilerParams(vmem_limit_bytes=40 << 20),
    )(*(list(chunks) * 3), cos_tab, sin_tab, seg_row[:, None], seg_row[None, :])


def attn_bwd(d_chunks, queries, key_rows, value_rows, att_out, lse_rows, cos_tab, sin_tab, seg_row):
    n_blk, blk = len(d_chunks), d_chunks[0].shape[0]
    rows = n_blk * blk
    n_head = 2
    lanes = n_head * HEAD_DIM
    width = queries.shape[1]
    n_pair = width // lanes
    wide = pl.BlockSpec((rows, lanes), lambda p: (0, p))
    return pl.pallas_call(
        functools.partial(attn_bwd_kernel, n_blk, n_head),
        grid=(n_pair,),
        in_specs=[pl.BlockSpec((blk, lanes), lambda p: (0, p))] * n_blk
        + [wide] * 4
        + [pl.BlockSpec((1, n_head, rows), lambda p: (p, 0, 0))]
        + table_specs(rows, lanes),
        out_specs=pl.BlockSpec((3, rows, lanes), lambda p: (0, 0, p)),
        out_shape=jax.ShapeDtypeStruct((3, rows, width), jnp.bfloat16),
        scratch_shapes=[
            pltpu.VMEM((rows, lanes), jnp.bfloat16),
            pltpu.VMEM((lanes, rows), jnp.bfloat16),
            pltpu.VMEM((rows, lanes), jnp.float32),
            pltpu.VMEM((rows, lanes), jnp.float32),
        ],
        cost_estimate=pl.CostEstimate(
            flops=10 * rows * rows * width, bytes_accessed=24 * rows * width, transcendentals=rows * rows * width // HEAD_DIM
        ),
        compiler_params=pltpu.CompilerParams(vmem_limit_bytes=40 << 20),
    )(*d_chunks, queries, key_rows, value_rows, att_out, lse_rows, cos_tab, sin_tab, seg_row[:, None], seg_row[None, :])


def dot_00(left, right):
    return lax.dot_general(left, right, (((0,), (0,)), ((), ())), preferred_element_type=jnp.float32)


def padded(n_rows, step):
    return -(-n_rows // step) * step


def with_rows(field_in, n_rows):
    return jnp.pad(field_in, ((0, n_rows - field_in.shape[0]), (0, 0)))


def after(first, later):
    return lax.optimization_barrier((first, later))[1]


def shards(hidden_in, segment_ids, gain_attn, gain_mlp, w_qkv, w_out, w_in, w_down, out_grad):
    n_tp = lax.axis_size("tensor")
    n_dp = lax.axis_size("dp")
    n_far = n_tp // 2
    shard_rows = hidden_in.shape[1]
    total_rows = shard_rows * n_tp
    model_width = hidden_in.shape[2]
    width = w_qkv.shape[2]
    ff = w_in.shape[2]
    me = lax.axis_index("tensor")
    my_dp = lax.axis_index("dp")
    bf = jnp.bfloat16

    def fetch(field_in, k):
        return lax.ppermute(field_in, "tensor", [((i + k) % n_tp, i) for i in range(n_tp)])

    def beside(field_in):
        return lax.ppermute(field_in, "tensor", [(i, i ^ 1) for i in range(n_tp)])

    rows_f = hidden_in[0].astype(jnp.float32)
    normed_attn, hat_attn, inv_attn = norm_fwd(rows_f, gain_attn)
    left, right = normed_attn, normed_attn
    from_right, from_left = [None], [None]
    for _ in range(1, n_tp):
        right = lax.ppermute(right, "tensor", [(i, i - 1) for i in range(1, n_tp)])
        left = lax.ppermute(left, "tensor", [(i, i + 1) for i in range(n_tp - 1)])
        from_right.append(right)
        from_left.append(left)
    blocks = [normed_attn] + [
        jnp.where(me + k < n_tp, from_right[k], from_left[n_tp - k]) for k in range(1, n_tp)
    ]
    order = sorted(range(1, n_tp), key=lambda k: (min(k, n_tp - k), k))

    w_in_t = jnp.transpose(w_in, (1, 2, 0))
    mlp_rows = jnp.concatenate([w_in_t[0], w_in_t[1], w_down], axis=0)
    pad_rows = padded(3 * ff, 16 * n_dp)
    part = pad_rows // n_dp
    my_part = lax.dynamic_slice_in_dim(with_rows(mlp_rows, pad_rows), my_dp * part, part, 0)
    out_part = w_out.shape[0] // n_dp
    my_out = lax.dynamic_slice_in_dim(w_out, my_dp * out_part, out_part, 0)
    far = [fetch(my_part, 2 * k) for k in range(1, n_far)]
    far += [fetch(my_out, k) for k in range(1, n_tp)]
    far = after((from_right[1], from_left[1]), jnp.concatenate(far, axis=0))
    far = lax.all_gather(far, "dp", axis=0, tiled=False)
    far_out = far[:, (n_far - 1) * part :].reshape(n_dp, n_tp - 1, out_part, model_width)
    far = [far[:, k * part : (k + 1) * part].reshape(pad_rows, model_width) for k in range(n_far - 1)]
    up_w = jnp.concatenate([w_in_t[0]] + [f[:ff] for f in far], axis=0)
    gate_w = jnp.concatenate([w_in_t[1]] + [f[ff : 2 * ff] for f in far], axis=0)
    down_w = jnp.concatenate([w_down] + [f[2 * ff : 3 * ff] for f in far], axis=0)
    out_rel = jnp.concatenate(
        [w_out, jnp.transpose(far_out, (1, 0, 2, 3)).reshape(-1, model_width)], axis=0
    )

    seg_can = segment_ids[0]
    seg_row = lax.dynamic_slice_in_dim(
        jnp.concatenate([seg_can, seg_can]), me * shard_rows, total_rows, 0
    )
    before = jnp.sum((seg_row[None, :] < seg_row[:, None]).astype(jnp.int32), axis=1)
    slots = (jnp.arange(total_rows, dtype=jnp.int32) + me * shard_rows) % total_rows
    cos_one, sin_one = rope_tables(slots - before, HEAD_DIM)
    cos_tab = jnp.tile(cos_one[0], (1, 2))
    sin_tab = jnp.tile(sin_one[0], (1, 2))
    valid_rows = (seg_row[:shard_rows] < total_rows).astype(jnp.float32)
    grad_top = out_grad[0].astype(jnp.float32) * valid_rows[:, None]
    grad_bf = grad_top.astype(bf)
    grad_other = beside(grad_bf)
    grad_pair = jnp.concatenate([grad_bf, grad_other], axis=0)

    w_two = w_qkv.reshape(model_width, 3 * width)
    chunks = [jnp.dot(b, w_two, preferred_element_type=jnp.float32) for b in blocks]
    queries, key_rows, value_rows, att_out, lse_rows = attn_fwd(
        chunks, cos_tab, sin_tab, seg_row, width
    )
    pieces = [att_out[:shard_rows]]
    for m in range(1, n_tp):
        k = n_tp - m
        pieces.append(fetch(att_out[k * shard_rows : (k + 1) * shard_rows], m))
    att_tok = jnp.concatenate(pieces, axis=1)
    mid_rows = rows_f + jnp.dot(att_tok, out_rel, preferred_element_type=jnp.float32)
    normed_mlp, hat_mlp, inv_mlp = norm_fwd(mid_rows, gain_mlp)
    pair_rows = jnp.concatenate([normed_mlp, beside(normed_mlp)], axis=0)

    up_part = dot_last(pair_rows, up_w)
    gate_part = dot_last(pair_rows, gate_w)
    act_up = gelu_val(up_part)
    mixed_act = (act_up * gate_part).astype(bf)
    d_mixed = dot_last(grad_pair, down_w)
    d_up = (d_mixed * gate_part * gelu_slope(up_part)).astype(bf)
    d_gate = (d_mixed * act_up).astype(bf)
    d_norm_part = (dot_mid(d_up, up_w) + dot_mid(d_gate, gate_w)).astype(bf)
    d_norm_other = beside(d_norm_part[shard_rows:])
    mixed_act = after(d_norm_part, mixed_act)
    mlp_part = dot_mid(mixed_act, down_w).astype(bf)

    grad_down_all = dot_00(mixed_act, grad_pair).astype(bf)
    grad_up_all = dot_00(d_up, pair_rows).astype(bf)
    grad_gate_all = dot_00(d_gate, pair_rows).astype(bf)
    full = padded(3 * ff, 32 * n_dp)
    sums = [
        jnp.concatenate(
            [g[k * ff : (k + 1) * ff] for g in (grad_up_all, grad_gate_all, grad_down_all)], axis=0
        )
        for k in range(n_far)
    ]
    sums = [with_rows(g, full).reshape(2, n_dp, -1, model_width) for g in sums]
    stacked = jnp.concatenate([g[h] for h in range(2) for g in sums], axis=1)
    stacked = stacked.reshape(-1, model_width)
    mlp_share = lax.psum_scatter(stacked, "dp", scatter_dimension=0, tiled=True)

    d_norm_mlp = d_norm_part[:shard_rows].astype(jnp.float32) + d_norm_other.astype(jnp.float32)
    gain_mlp_part = jnp.sum(d_norm_mlp * hat_mlp, axis=0)
    d_mid = grad_top + norm_bwd(d_norm_mlp, hat_mlp, inv_mlp, gain_mlp)
    d_mid_bf = d_mid.astype(bf)
    d_att = dot_last(d_mid_bf, out_rel).astype(bf)
    d_chunks = [d_att[:, :width]] + [None] * (n_tp - 1)
    for m in range(1, n_tp):
        d_chunks[n_tp - m] = fetch(d_att[:, m * width : (m + 1) * width], n_tp - m)
    grad_out_all = dot_00(att_tok, d_mid_bf).astype(bf)
    mlp_other = beside(after(d_chunks[-1], mlp_part[shard_rows:]))
    final_rows = (
        mid_rows + mlp_part[:shard_rows].astype(jnp.float32) + mlp_other.astype(jnp.float32)
    ).astype(bf)

    d_proj = attn_bwd(
        d_chunks, queries, key_rows, value_rows, att_out, lse_rows, cos_tab, sin_tab, seg_row
    )
    mlp_share = after(d_proj, mlp_share).reshape(2, 1, -1, model_width)
    w_three = jnp.transpose(w_qkv, (1, 0, 2))

    def back_rows(k):
        rows = d_proj[:, k * shard_rows : (k + 1) * shard_rows]
        total = sum(dot_last(rows[s], w_three[s]) for s in range(3))
        return total.astype(bf)

    gain_attn_part = jnp.zeros((model_width,), jnp.float32)
    got = []
    for k in order + [0]:
        mine = back_rows(k)
        gain_attn_part = gain_attn_part + jnp.sum(
            mine.astype(jnp.float32) * blocks[k].astype(jnp.float32), axis=0
        )
        got.append(mine if k == 0 else fetch(mine, n_tp - k))
    gathered = jnp.concatenate(blocks, axis=0)
    grad_qkv = [dot_00(gathered, d_proj[s]).astype(bf) for s in range(3)]
    out_blocks = [grad_out_all[m * width : (m + 1) * width] for m in range(n_tp)]
    out_hops = tuple(range(n_tp))
    if width % (32 * n_dp):
        out_total = out_blocks[0].astype(jnp.float32)
        for m in out_hops[1:]:
            out_total = out_total + fetch(out_blocks[m], n_tp - m).astype(jnp.float32)
        out_blocks, out_hops = [out_total.astype(bf)], (0,)
    hops = tuple(2 * k for k in range(n_far))
    (*grad_qkv, grad_out_w), (mlp_total,) = grad_reduce(
        [[g] for g in grad_qkv]
        + [out_blocks],
        ((0,),) * 3 + (out_hops,),
        [mlp_share],
        (hops,),
        1,
    )
    mlp_total = mlp_total.reshape(full, model_width)
    grad_in = jnp.transpose(mlp_total[: 2 * ff].reshape(2, ff, model_width), (2, 0, 1))
    grad_down = mlp_total[2 * ff : 3 * ff]
    grad_qkv = jnp.stack(grad_qkv, axis=1)
    gain_both = gain_reduce(jnp.stack([gain_attn_part / gain_attn, gain_mlp_part]), 3)
    *got, mlp_total, gain_both = lax.optimization_barrier((*got, mlp_total, gain_both))
    d_norm_attn = sum(g.astype(jnp.float32) for g in got)
    d_rows = d_mid + norm_bwd(d_norm_attn, hat_attn, inv_attn, gain_attn)
    return (
        final_rows[None],
        d_rows[None],
        gain_both[0],
        gain_both[1],
        grad_qkv,
        grad_out_w,
        grad_in,
        grad_down,
    )


def solution(mesh):
    return jax.shard_map(
        shards,
        mesh=mesh,
        in_specs=(
            P("dp", "tensor", None),
            P("dp", None),
            P(),
            P(),
            P(None, None, "tensor"),
            P("tensor", None),
            P(None, None, "tensor"),
            P("tensor", None),
            P("dp", "tensor", None),
        ),
        out_specs=(
            P("dp", "tensor", None),
            P("dp", "tensor", None),
            P("tensor"),
            P("tensor"),
            P(None, None, "tensor"),
            P("tensor", None),
            P(None, None, "tensor"),
            P("tensor", None),
        ),
        check_vma=False,
    )
```

```python
import functools
import math

import jax
import jax.numpy as jnp
from jax import lax
from jax.experimental import pallas as pl
from jax.experimental.pallas import tpu as pltpu
from jax.sharding import PartitionSpec as P


HEAD_DIM = 64


eps_norm = 1e-05
rope_theta = 160000.0
neg_fill = -1e30
sqrt_half = 0.7071067811865476
inv_sqrt_two_pi = 0.3989422804014327


def norm_fwd(rows_f, gain_vec):
    mean_row = jnp.mean(rows_f, axis=-1, keepdims=True)
    centred = rows_f - mean_row
    var_row = jnp.mean(centred * centred, axis=-1, keepdims=True)
    inv_std = lax.rsqrt(var_row + eps_norm)
    hat_rows = centred * inv_std
    return ((hat_rows * gain_vec).astype(jnp.bfloat16), hat_rows, inv_std)


def norm_bwd(grad_norm, hat_rows, inv_std, gain_vec):
    grad_hat = grad_norm * gain_vec
    mean_one = jnp.mean(grad_hat, axis=-1, keepdims=True)
    mean_two = jnp.mean(grad_hat * hat_rows, axis=-1, keepdims=True)
    return inv_std * (grad_hat - mean_one - hat_rows * mean_two)


def rope_tables(positions, head_dim):
    half_dim = head_dim // 2
    inv_freq = jnp.exp(
        jnp.arange(half_dim, dtype=jnp.float32) * (-2.0 * math.log(rope_theta) / head_dim)
    )
    angles = positions.astype(jnp.float32)[:, None] * inv_freq[None, :]
    cos_tab = jnp.concatenate([jnp.cos(angles), jnp.cos(angles)], axis=-1)
    sin_tab = jnp.concatenate([jnp.sin(angles), jnp.sin(angles)], axis=-1)
    return (cos_tab[None], sin_tab[None])


def gelu_val(field_in):
    return 0.5 * field_in * (1.0 + lax.erf(field_in * sqrt_half))


def gelu_slope(field_in):
    return (
        0.5 * (1.0 + lax.erf(field_in * sqrt_half))
        + field_in * jnp.exp(-0.5 * field_in * field_in) * inv_sqrt_two_pi
    )


def bit_orders(n_dp):
    bits = [1 << i for i in range(n_dp.bit_length() - 1)]
    rest = bits[1:]
    turn = len(rest) // 2
    return (bits, bits[:1] + rest[turn:] + rest[:turn])


def grad_reduce_kernel(n_dp, n_tp, shifts, splits, *refs):
    orders = bit_orders(n_dp)
    n_stage = len(orders[0])
    n_arr = len(shifts)
    whole = [row is None for row in splits]
    x_refs = refs[:n_arr]
    pos = n_arr
    out_refs = []
    for row in splits:
        count = 1 if row is None else len(row)
        out_refs.append(refs[pos : pos + count])
        pos += count
    gath = refs[pos : pos + n_arr]
    pos += n_arr
    recv, work, far = {}, {}, {}
    for arr in range(n_arr):
        if whole[arr]:
            for stage in range(n_stage):
                recv[arr, stage] = refs[pos]
                pos += 1
            for stage in range(n_stage):
                work[arr, stage] = refs[pos]
                pos += 1
        if len(shifts[arr]) > 1:
            far[arr] = refs[pos]
            pos += 1
    send_sem, recv_sem, far_send, far_recv = refs[pos : pos + 4]
    me = lax.axis_index("dp")
    mine = lax.axis_index("tensor")
    mesh_type = pl.DeviceIdType.MESH

    def bit_of(bit):
        return lax.rem(me // bit, 2)

    def partner_of(bit):
        return me + bit - 2 * bit * bit_of(bit)

    pending = []

    def remote(src, dst, step, half, arr, bit):
        copy = pltpu.make_async_remote_copy(
            src_ref=src,
            dst_ref=dst,
            send_sem=send_sem.at[step, half, arr],
            recv_sem=recv_sem.at[step, half, arr],
            device_id=(partner_of(bit), mine),
            device_id_type=mesh_type,
        )
        copy.start()
        pending.append(copy)
        return copy

    steps = {s for row in shifts for s in row if s}
    steps = sorted(steps | {n_tp - s for s in steps})
    barrier = pltpu.get_barrier_semaphore()
    for bit in orders[0]:
        pl.semaphore_signal(barrier, inc=1, device_id=(partner_of(bit), mine), device_id_type=mesh_type)
    for s in steps:
        pl.semaphore_signal(
            barrier, inc=1, device_id=(me, lax.rem(mine + s, n_tp)), device_id_type=mesh_type
        )
    pl.semaphore_wait(barrier, n_stage + len(steps))

    offs = [[0], [0]]
    for half in range(2):
        for stage in range(n_stage):
            bit = orders[half][stage]
            offs[half].append(offs[half][-1] + bit_of(bit) * (n_dp >> (stage + 1)))

    def source(arr, stage):
        return x_refs[arr] if stage == 0 else work[arr, stage - 1]

    def start_sum(arr, half, stage):
        bit = orders[half][stage]
        size = n_dp >> (stage + 1)
        away = (1 - bit_of(bit)) * size
        src = source(arr, stage).at[half, pl.ds(away, size)]
        return remote(src, recv[arr, stage].at[half], stage, half, arr, bit)

    def own_piece(arr, half):
        if whole[arr]:
            return work[arr, n_stage - 1].at[half, 0]
        return x_refs[arr].at[half, 0]

    def start_far(arr, half):
        part = gath[arr].shape[2]
        copies = []
        for b in range(1, len(shifts[arr])):
            copy = pltpu.make_async_remote_copy(
                src_ref=own_piece(arr, half).at[pl.ds(b * part, part)],
                dst_ref=far[arr].at[b - 1, half],
                send_sem=far_send.at[arr, b, half],
                recv_sem=far_recv.at[arr, b, half],
                device_id=(me, lax.rem(mine + shifts[arr][b], n_tp)),
                device_id_type=mesh_type,
            )
            copy.start()
            pending.append(copy)
            copies.append(copy)
        return copies

    def start_spread(arr, half, stage):
        size = n_dp >> (stage + 1)
        part = gath[arr].at[half, pl.ds(offs[half][stage + 1], size)]
        return remote(part, part, n_stage + stage, half, arr, orders[half][stage])

    def finish_sum(arr, half, stage, copy):
        size = n_dp >> (stage + 1)
        kept = bit_of(orders[half][stage]) * size
        copy.wait_recv()
        src, got, dst = source(arr, stage), recv[arr, stage], work[arr, stage]

        def add_one(i, carry):
            total = src[half, kept + i].astype(jnp.float32) + got[half, i].astype(jnp.float32)
            dst[half, i] = total.astype(jnp.bfloat16)
            return carry

        lax.fori_loop(0, size, add_one, 0)

    def finish_far(arr, half, copies):
        part = gath[arr].shape[2]
        total = own_piece(arr, half)[pl.ds(0, part)].astype(jnp.float32)
        for b, copy in enumerate(copies):
            copy.wait_recv()
            total = total + far[arr][b, half].astype(jnp.float32)
        gath[arr][half, offs[half][-1]] = total.astype(jnp.bfloat16)

    order = [(arr, half) for arr in range(n_arr) for half in range(2)]
    flying = {}
    for key in order:
        flying[key] = start_sum(*key, 0) if whole[key[0]] else start_far(*key)
    for stage in range(n_stage):
        for arr, half in order:
            if whole[arr]:
                finish_sum(arr, half, stage, flying[arr, half])
                if stage + 1 < n_stage:
                    flying[arr, half] = start_sum(arr, half, stage + 1)
                else:
                    flying[arr, half] = start_far(arr, half)
    for arr, half in order:
        finish_far(arr, half, flying[arr, half])
        flying[arr, half] = start_spread(arr, half, n_stage - 1)
    for stage in reversed(range(n_stage)):
        for arr, half in order:
            flying[arr, half].wait_recv()
            if stage:
                flying[arr, half] = start_spread(arr, half, stage - 1)
    for arr, half in order:
        if whole[arr]:

            def move_one(i, carry, arr=arr, half=half):
                out_refs[arr][0][half, i] = gath[arr][half, i].astype(jnp.float32)
                return carry

            lax.fori_loop(0, n_dp, move_one, 0)
        else:
            part = gath[arr].shape[2]
            for i in range(n_dp):
                slot = 0
                for stage in range(n_stage):
                    slot += (i // orders[half][stage]) % 2 * (n_dp >> (stage + 1))
                begin = (half * n_dp + i) * part
                low = 0
                for out_ref, rows in zip(out_refs[arr], splits[arr]):
                    first, last = max(begin, low), min(begin + part, low + rows)
                    if first < last:
                        out_ref[first - low : last - low] = gath[arr][
                            half, slot, first - begin : last - begin
                        ].astype(jnp.float32)
                    low += rows
    for copy in pending:
        copy.wait_send()


def grad_reduce(grads, shifts, shares, share_shifts, share_splits, call_id):
    n_dp = lax.axis_size("dp")
    n_tp = lax.axis_size("tensor")
    n_stage = n_dp.bit_length() - 1
    bf = jnp.bfloat16
    args, cols, parts, rows_of = [], [], [], []
    for blocks in grads:
        rows, c = blocks[0].shape
        full = padded(rows, 32 * n_dp)
        part = full // (2 * n_dp)
        args.append(
            jnp.concatenate(
                [with_rows(g, full).reshape(2, n_dp, part, c) for g in blocks], axis=2
            ).astype(bf)
        )
        cols.append(c)
        parts.append(part)
        rows_of.append(rows)
    for share, row in zip(shares, share_shifts):
        args.append(share)
        cols.append(share.shape[-1])
        parts.append(share.shape[2] // len(row))
    shifts = tuple(shifts) + tuple(share_shifts)
    splits = (None,) * len(grads) + tuple(share_splits)
    scratch = [pltpu.VMEM((2, n_dp, p, c), bf) for p, c in zip(parts, cols)]
    for row, p, c, split in zip(shifts, parts, cols, splits):
        if split is None:
            for _ in range(2):
                for stage in range(n_stage):
                    scratch.append(pltpu.VMEM((2, n_dp >> (stage + 1), len(row) * p, c), bf))
        if len(row) > 1:
            scratch.append(pltpu.VMEM((len(row) - 1, 2, p, c), bf))
    most = max(len(row) for row in shifts)
    scratch += [pltpu.SemaphoreType.DMA((2 * n_stage, 2, len(args)))] * 2
    scratch += [pltpu.SemaphoreType.DMA((len(args), most, 2))] * 2
    moved = sum(4 * n_dp * len(row) * p * c for row, p, c in zip(shifts, parts, cols))
    out_shape = []
    for p, c, split in zip(parts, cols, splits):
        shapes = [(2, n_dp, p, c)] if split is None else [(r, c) for r in split]
        out_shape += [jax.ShapeDtypeStruct(shape, jnp.float32) for shape in shapes]
    done = pl.pallas_call(
        functools.partial(grad_reduce_kernel, n_dp, n_tp, shifts, splits),
        out_shape=out_shape,
        in_specs=[pl.BlockSpec(memory_space=pltpu.VMEM)] * len(args),
        out_specs=[pl.BlockSpec(memory_space=pltpu.VMEM)] * len(out_shape),
        scratch_shapes=scratch,
        cost_estimate=pl.CostEstimate(flops=0, bytes_accessed=30 * moved, transcendentals=0),
        compiler_params=pltpu.CompilerParams(
            collective_id=call_id, has_side_effects=True, vmem_limit_bytes=48 << 20
        ),
    )(*args)
    totals = [o.reshape(-1, c)[:rows] for o, c, rows in zip(done, cols, rows_of)]
    return totals, done[len(grads) :]


def turn_lanes(field_in, half_dim):
    lanes = lax.broadcasted_iota(jnp.int32, field_in.shape, 1)
    width = field_in.shape[1]
    low = lanes % (2 * half_dim) < half_dim
    ahead = pltpu.roll(field_in, width - half_dim, 1)
    behind = pltpu.roll(field_in, half_dim, 1)
    return jnp.where(low, -ahead, behind)


def head_mask(shape, head):
    return lax.broadcasted_iota(jnp.int32, shape, 1) // HEAD_DIM == head


def dot_last(left, right):
    return lax.dot_general(left, right, (((1,), (1,)), ((), ())), preferred_element_type=jnp.float32)


def dot_mid(left, right):
    return lax.dot_general(left, right, (((1,), (0,)), ((), ())), preferred_element_type=jnp.float32)


def attn_fwd_kernel(n_blk, n_head, *refs):
    q_in, k_in, v_in = refs[:n_blk], refs[n_blk : 2 * n_blk], refs[2 * n_blk : 3 * n_blk]
    cos_ref, sin_ref, segc_ref, segr_ref = refs[3 * n_blk : 3 * n_blk + 4]
    q_ref, k_ref, v_ref, att_ref, lse_ref, vt_ref = refs[3 * n_blk + 4 :]
    blk = q_in[0].shape[0]
    half_dim = HEAD_DIM // 2
    scale_val = 1.0 / math.sqrt(HEAD_DIM)
    for c in range(n_blk):
        rows = pl.ds(c * blk, blk)
        cos_tab, sin_tab = cos_ref[rows], sin_ref[rows]
        for src, dst in ((q_in[c], q_ref), (k_in[c], k_ref)):
            z = src[...]
            dst[rows] = (z * cos_tab + turn_lanes(z, half_dim) * sin_tab).astype(jnp.bfloat16)
        value = v_in[c][...]
        v_ref[rows] = value.astype(jnp.bfloat16)
        vt_ref[:, rows] = jnp.transpose(value).astype(jnp.bfloat16)

    def one_block(i, carry):
        rows = pl.ds(pl.multiple_of(i * blk, blk), blk)
        query = q_ref[rows]
        same_doc = segc_ref[...] == segr_ref[:, rows]
        parts = []
        for h in range(n_head):
            masked = jnp.where(head_mask(query.shape, h), query, jnp.zeros_like(query))
            scores = jnp.where(same_doc, dot_last(k_ref[...], masked) * scale_val, neg_fill)
            top = jnp.max(scores, axis=0, keepdims=True)
            exp_vals = jnp.exp(scores - top)
            total = jnp.sum(exp_vals, axis=0, keepdims=True)
            prob_bf = (exp_vals * (1.0 / total)).astype(jnp.bfloat16)
            parts.append(dot_mid(vt_ref[h * HEAD_DIM : (h + 1) * HEAD_DIM], prob_bf))
            lse_ref[0, h : h + 1, rows] = top + jnp.log(total)
        out = jnp.transpose(jnp.concatenate(parts, axis=0))
        att_ref[rows] = out.astype(jnp.bfloat16)
        return carry

    lax.fori_loop(0, n_blk, one_block, 0)


def attn_bwd_kernel(n_blk, n_head, *refs):
    d_in = refs[:n_blk]
    q_ref, k_ref, v_ref, att_ref, lse_ref, cos_ref, sin_ref, segc_ref, segr_ref = refs[n_blk : n_blk + 9]
    out_ref, d_ref, kt_ref, dk_ref, dv_ref = refs[n_blk + 9 :]
    blk = d_in[0].shape[0]
    half_dim = HEAD_DIM // 2
    scale_val = 1.0 / math.sqrt(HEAD_DIM)
    for c in range(n_blk):
        rows = pl.ds(c * blk, blk)
        d_ref[rows] = d_in[c][...]
        kt_ref[:, rows] = jnp.transpose(k_ref[rows].astype(jnp.float32)).astype(jnp.bfloat16)
    dk_ref[...] = jnp.zeros_like(dk_ref)
    dv_ref[...] = jnp.zeros_like(dv_ref)

    def back_turn(grad, rows):
        turned = turn_lanes(grad * sin_ref[rows], half_dim)
        return (grad * cos_ref[rows] - turned).astype(jnp.bfloat16)

    def one_block(i, carry):
        rows = pl.ds(pl.multiple_of(i * blk, blk), blk)
        query, d_att = q_ref[rows], d_ref[rows]
        both = jnp.transpose(d_att.astype(jnp.float32) * att_ref[rows].astype(jnp.float32))
        same_doc = segc_ref[...] == segr_ref[:, rows]
        parts = []
        for h in range(n_head):
            own = head_mask(query.shape, h)
            q_h = jnp.where(own, query, jnp.zeros_like(query))
            d_h = jnp.where(own, d_att, jnp.zeros_like(d_att))
            delta = jnp.sum(both[h * HEAD_DIM : (h + 1) * HEAD_DIM], axis=0, keepdims=True)
            scores = jnp.where(same_doc, dot_last(k_ref[...], q_h) * scale_val, neg_fill)
            prob_f = jnp.exp(scores - lse_ref[0, h : h + 1, rows])
            grad_prob = dot_last(v_ref[...], d_h)
            score_bf = (prob_f * (grad_prob - delta)).astype(jnp.bfloat16)
            dv_ref[...] += dot_mid(prob_f.astype(jnp.bfloat16), d_h)
            dk_ref[...] += dot_mid(score_bf, q_h)
            parts.append(dot_mid(kt_ref[h * HEAD_DIM : (h + 1) * HEAD_DIM], score_bf))
        grad_query = jnp.transpose(jnp.concatenate(parts, axis=0)) * scale_val
        out_ref[0, rows] = back_turn(grad_query, rows)
        return carry

    lax.fori_loop(0, n_blk, one_block, 0)
    for c in range(n_blk):
        rows = pl.ds(c * blk, blk)
        out_ref[1, rows] = back_turn(dk_ref[rows] * scale_val, rows)
        out_ref[2, rows] = dv_ref[rows].astype(jnp.bfloat16)


def table_specs(rows, lanes):
    return [
        pl.BlockSpec((rows, lanes), lambda p: (0, 0)),
        pl.BlockSpec((rows, lanes), lambda p: (0, 0)),
        pl.BlockSpec((rows, 1), lambda p: (0, 0)),
        pl.BlockSpec((1, rows), lambda p: (0, 0)),
    ]


def attn_fwd(chunks, cos_tab, sin_tab, seg_row, width):
    n_blk, blk = len(chunks), chunks[0].shape[0]
    rows = n_blk * blk
    n_head = 2
    lanes = n_head * HEAD_DIM
    n_pair = width // lanes

    def at(s):
        return pl.BlockSpec((blk, lanes), lambda p: (0, s * n_pair + p))

    wide = pl.BlockSpec((rows, lanes), lambda p: (0, p))
    flat = jax.ShapeDtypeStruct((rows, width), jnp.bfloat16)
    return pl.pallas_call(
        functools.partial(attn_fwd_kernel, n_blk, n_head),
        grid=(n_pair,),
        in_specs=[at(s) for s in range(3) for _ in range(n_blk)] + table_specs(rows, lanes),
        out_specs=[wide, wide, wide, wide, pl.BlockSpec((1, n_head, rows), lambda p: (p, 0, 0))],
        out_shape=[flat] * 4 + [jax.ShapeDtypeStruct((n_pair, n_head, rows), jnp.float32)],
        scratch_shapes=[pltpu.VMEM((lanes, rows), jnp.bfloat16)],
        cost_estimate=pl.CostEstimate(
            flops=4 * rows * rows * width, bytes_accessed=24 * rows * width, transcendentals=rows * rows * width // HEAD_DIM
        ),
        compiler_params=pltpu.CompilerParams(vmem_limit_bytes=40 << 20),
    )(*(list(chunks) * 3), cos_tab, sin_tab, seg_row[:, None], seg_row[None, :])


def attn_bwd(d_chunks, queries, key_rows, value_rows, att_out, lse_rows, cos_tab, sin_tab, seg_row):
    n_blk, blk = len(d_chunks), d_chunks[0].shape[0]
    rows = n_blk * blk
    n_head = 2
    lanes = n_head * HEAD_DIM
    width = queries.shape[1]
    n_pair = width // lanes
    wide = pl.BlockSpec((rows, lanes), lambda p: (0, p))
    return pl.pallas_call(
        functools.partial(attn_bwd_kernel, n_blk, n_head),
        grid=(n_pair,),
        in_specs=[pl.BlockSpec((blk, lanes), lambda p: (0, p))] * n_blk
        + [wide] * 4
        + [pl.BlockSpec((1, n_head, rows), lambda p: (p, 0, 0))]
        + table_specs(rows, lanes),
        out_specs=pl.BlockSpec((3, rows, lanes), lambda p: (0, 0, p)),
        out_shape=jax.ShapeDtypeStruct((3, rows, width), jnp.bfloat16),
        scratch_shapes=[
            pltpu.VMEM((rows, lanes), jnp.bfloat16),
            pltpu.VMEM((lanes, rows), jnp.bfloat16),
            pltpu.VMEM((rows, lanes), jnp.float32),
            pltpu.VMEM((rows, lanes), jnp.float32),
        ],
        cost_estimate=pl.CostEstimate(
            flops=10 * rows * rows * width, bytes_accessed=24 * rows * width, transcendentals=rows * rows * width // HEAD_DIM
        ),
        compiler_params=pltpu.CompilerParams(vmem_limit_bytes=40 << 20),
    )(*d_chunks, queries, key_rows, value_rows, att_out, lse_rows, cos_tab, sin_tab, seg_row[:, None], seg_row[None, :])


def dot_00(left, right):
    return lax.dot_general(left, right, (((0,), (0,)), ((), ())), preferred_element_type=jnp.float32)


def padded(n_rows, step):
    return -(-n_rows // step) * step


def with_rows(field_in, n_rows):
    return jnp.pad(field_in, ((0, n_rows - field_in.shape[0]), (0, 0)))


def after(first, later):
    return lax.optimization_barrier((first, later))[1]


def shards(hidden_in, segment_ids, gain_attn, gain_mlp, w_qkv, w_out, w_in, w_down, out_grad):
    n_tp = lax.axis_size("tensor")
    n_dp = lax.axis_size("dp")
    n_far = n_tp // 2
    shard_rows = hidden_in.shape[1]
    total_rows = shard_rows * n_tp
    model_width = hidden_in.shape[2]
    width = w_qkv.shape[2]
    ff = w_in.shape[2]
    me = lax.axis_index("tensor")
    my_dp = lax.axis_index("dp")
    bf = jnp.bfloat16

    def fetch(field_in, k):
        return lax.ppermute(field_in, "tensor", [((i + k) % n_tp, i) for i in range(n_tp)])

    def beside(field_in):
        return lax.ppermute(field_in, "tensor", [(i, i ^ 1) for i in range(n_tp)])

    rows_f = hidden_in[0].astype(jnp.float32)
    normed_attn, hat_attn, inv_attn = norm_fwd(rows_f, gain_attn)
    blocks = [normed_attn] + [None] * (n_tp - 1)
    order = sorted(range(1, n_tp), key=lambda k: (min(k, n_tp - k), k))
    for k in order:
        blocks[k] = fetch(normed_attn, k)

    w_in_t = jnp.transpose(w_in, (1, 2, 0))
    mlp_rows = jnp.concatenate([w_in_t[0], w_in_t[1], w_down], axis=0)
    pad_rows = padded(3 * ff, 16 * n_dp)
    part = pad_rows // n_dp
    my_part = lax.dynamic_slice_in_dim(with_rows(mlp_rows, pad_rows), my_dp * part, part, 0)
    out_part = w_out.shape[0] // n_dp
    my_out = lax.dynamic_slice_in_dim(w_out, my_dp * out_part, out_part, 0)
    far = [fetch(my_part, 2 * k) for k in range(1, n_far)]
    far += [fetch(my_out, k) for k in range(1, n_tp)]
    far = lax.all_gather(jnp.concatenate(far, axis=0), "dp", axis=0, tiled=False)
    far_out = far[:, (n_far - 1) * part :].reshape(n_dp, n_tp - 1, out_part, model_width)
    far = [far[:, k * part : (k + 1) * part].reshape(pad_rows, model_width) for k in range(n_far - 1)]
    up_w = jnp.concatenate([w_in_t[0]] + [f[:ff] for f in far], axis=0)
    gate_w = jnp.concatenate([w_in_t[1]] + [f[ff : 2 * ff] for f in far], axis=0)
    down_w = jnp.concatenate([w_down] + [f[2 * ff : 3 * ff] for f in far], axis=0)
    out_rel = jnp.concatenate(
        [w_out, jnp.transpose(far_out, (1, 0, 2, 3)).reshape(-1, model_width)], axis=0
    )

    seg_can = segment_ids[0]
    seg_row = lax.dynamic_slice_in_dim(
        jnp.concatenate([seg_can, seg_can]), me * shard_rows, total_rows, 0
    )
    before = jnp.sum((seg_row[None, :] < seg_row[:, None]).astype(jnp.int32), axis=1)
    slots = (jnp.arange(total_rows, dtype=jnp.int32) + me * shard_rows) % total_rows
    cos_one, sin_one = rope_tables(slots - before, HEAD_DIM)
    cos_tab = jnp.tile(cos_one[0], (1, 2))
    sin_tab = jnp.tile(sin_one[0], (1, 2))
    valid_rows = (seg_row[:shard_rows] < total_rows).astype(jnp.float32)
    grad_top = out_grad[0].astype(jnp.float32) * valid_rows[:, None]
    grad_bf = grad_top.astype(bf)
    grad_other = beside(grad_bf)
    grad_pair = jnp.concatenate([grad_bf, grad_other], axis=0)

    w_two = w_qkv.reshape(model_width, 3 * width)
    chunks = [jnp.dot(b, w_two, preferred_element_type=jnp.float32) for b in blocks]
    queries, key_rows, value_rows, att_out, lse_rows = attn_fwd(
        chunks, cos_tab, sin_tab, seg_row, width
    )
    pieces = [att_out[:shard_rows]]
    for m in range(1, n_tp):
        k = n_tp - m
        pieces.append(fetch(att_out[k * shard_rows : (k + 1) * shard_rows], m))
    att_tok = jnp.concatenate(pieces, axis=1)
    mid_rows = rows_f + jnp.dot(att_tok, out_rel, preferred_element_type=jnp.float32)
    normed_mlp, hat_mlp, inv_mlp = norm_fwd(mid_rows, gain_mlp)
    pair_rows = jnp.concatenate([normed_mlp, beside(normed_mlp)], axis=0)

    up_part = dot_last(pair_rows, up_w)
    gate_part = dot_last(pair_rows, gate_w)
    act_up = gelu_val(up_part)
    mixed_act = (act_up * gate_part).astype(bf)
    d_mixed = dot_last(grad_pair, down_w)
    d_up = (d_mixed * gate_part * gelu_slope(up_part)).astype(bf)
    d_gate = (d_mixed * act_up).astype(bf)
    d_norm_part = (dot_mid(d_up, up_w) + dot_mid(d_gate, gate_w)).astype(bf)
    d_norm_send = d_norm_part[shard_rows:]
    d_norm_other = beside(d_norm_send)
    mixed_act, d_up, d_gate = lax.optimization_barrier((d_norm_send, mixed_act, d_up, d_gate))[1:]

    grad_down_all = dot_00(mixed_act, grad_pair).astype(bf)
    grad_up_all = dot_00(d_up, pair_rows).astype(bf)
    grad_gate_all = dot_00(d_gate, pair_rows).astype(bf)
    full = padded(3 * ff, 32 * n_dp)
    sums = [
        jnp.concatenate(
            [g[k * ff : (k + 1) * ff] for g in (grad_up_all, grad_gate_all, grad_down_all)], axis=0
        )
        for k in range(n_far)
    ]
    sums = [with_rows(g, full).reshape(2, n_dp, -1, model_width) for g in sums]
    stacked = jnp.concatenate([g[h] for h in range(2) for g in sums], axis=1)
    stacked = stacked.reshape(-1, model_width)
    mlp_share = lax.psum_scatter(stacked, "dp", scatter_dimension=0, tiled=True)

    d_norm_mlp = d_norm_part[:shard_rows].astype(jnp.float32) + d_norm_other.astype(jnp.float32)
    gain_mlp_part = jnp.sum(d_norm_mlp * hat_mlp, axis=0)
    d_mid = grad_top + norm_bwd(d_norm_mlp, hat_mlp, inv_mlp, gain_mlp)
    d_mid_bf = d_mid.astype(bf)
    d_att = dot_last(d_mid_bf, out_rel).astype(bf)
    d_chunks = [d_att[:, :width]] + [None] * (n_tp - 1)
    for m in range(1, n_tp):
        d_chunks[n_tp - m] = fetch(d_att[:, m * width : (m + 1) * width], n_tp - m)
    grad_out_all = dot_00(att_tok, d_mid_bf).astype(bf)
    mlp_part = dot_mid(after(d_att, mixed_act), down_w).astype(bf)
    mlp_other = beside(mlp_part[shard_rows:])
    final_rows = (
        mid_rows + mlp_part[:shard_rows].astype(jnp.float32) + mlp_other.astype(jnp.float32)
    ).astype(bf)

    d_proj = attn_bwd(
        d_chunks, queries, key_rows, value_rows, att_out, lse_rows, cos_tab, sin_tab, seg_row
    )
    mlp_share = after(d_proj, mlp_share).reshape(2, 1, -1, model_width)
    w_three = jnp.transpose(w_qkv, (1, 0, 2))

    def back_rows(k):
        rows = d_proj[:, k * shard_rows : (k + 1) * shard_rows]
        total = sum(dot_last(rows[s], w_three[s]) for s in range(3))
        return total.astype(bf)

    gain_attn_part = jnp.zeros((model_width,), jnp.float32)
    got = []
    for k in order + [0]:
        mine = back_rows(k)
        gain_attn_part = gain_attn_part + jnp.sum(
            mine.astype(jnp.float32) * blocks[k].astype(jnp.float32), axis=0
        )
        got.append(mine if k == 0 else fetch(mine, n_tp - k))
    gathered = jnp.concatenate(blocks, axis=0)
    grad_qkv = [dot_00(gathered, d_proj[s]).astype(bf) for s in range(3)]
    out_blocks = [grad_out_all[m * width : (m + 1) * width] for m in range(n_tp)]
    out_hops = tuple(range(n_tp))
    if width % (32 * n_dp):
        out_total = out_blocks[0].astype(jnp.float32)
        for m in out_hops[1:]:
            out_total = out_total + fetch(out_blocks[m], n_tp - m).astype(jnp.float32)
        out_blocks, out_hops = [out_total.astype(bf)], (0,)
    hops = tuple(2 * k for k in range(n_far))
    gains = jnp.stack([gain_attn_part / gain_attn, gain_mlp_part], axis=1)
    gains = jnp.pad(gains.astype(bf), ((0, 0), (0, 126)))
    gain_blocks = [
        lax.dynamic_slice_in_dim(gains, (me + m) % n_tp * width, width, 0) for m in range(n_tp)
    ]
    (*grad_qkv, grad_out_w, gain_both), (grad_in, grad_down) = grad_reduce(
        [[g] for g in grad_qkv] + [out_blocks, gain_blocks],
        ((0,),) * 3 + (out_hops, tuple(range(n_tp))),
        [mlp_share],
        (hops,),
        ((2 * ff, ff),),
        1,
    )
    grad_qkv = jnp.stack(grad_qkv, axis=1)
    *got, grad_in, gain_both = lax.optimization_barrier((*got, grad_in, gain_both))
    grad_in = jnp.transpose(grad_in.reshape(2, ff, model_width), (2, 0, 1))
    d_norm_attn = sum(g.astype(jnp.float32) for g in got)
    d_rows = d_mid + norm_bwd(d_norm_attn, hat_attn, inv_attn, gain_attn)
    return (
        final_rows[None],
        d_rows[None],
        gain_both[:, 0],
        gain_both[:, 1],
        grad_qkv,
        grad_out_w,
        grad_in,
        grad_down,
    )


def solution(mesh):
    return jax.shard_map(
        shards,
        mesh=mesh,
        in_specs=(
            P("dp", "tensor", None),
            P("dp", None),
            P(),
            P(),
            P(None, None, "tensor"),
            P("tensor", None),
            P(None, None, "tensor"),
            P("tensor", None),
            P("dp", "tensor", None),
        ),
        out_specs=(
            P("dp", "tensor", None),
            P("dp", "tensor", None),
            P("tensor"),
            P("tensor"),
            P(None, None, "tensor"),
            P("tensor", None),
            P(None, None, "tensor"),
            P("tensor", None),
        ),
        check_vma=False,
    )
```
